32 devices in a mesh: segment: 2 (over x), seq: 16 (over z, y, core).
Axes of the slice: x: 2, y: 2, z: 4, core: 2. Of those that a mesh axis runs over, the one named last changes fastest.
Arguments:
- queries: bfloat16 [2, 1024, 1536], P('segment', 'seq'), may hold values from -10 to 10
- key_value: bfloat16 [2, 2, 1024, 1536], P(None, 'segment', 'seq'), may hold values from -10 to 10
Outputs:
- handed: bfloat16 [2, 1024, 1536], P('segment', 'seq')
The draws below stay inside these ranges and needn't reach their ends.
All inputs are finite; a program needn't handle non-finite values.
Results may differ from the reference program's by a relative error of at most 0.0065.
Values may be sent and summed in bfloat16 or wider, within the bound.
No kernel may reach another device: no remote copies, remote signals or barrier semaphores. Data moves between devices by JAX's collectives and lax.ppermute only.
A program may use at most 64 MiB of HBM per device.

```python
import jax
import jax.numpy as jnp
from jax import lax

HEADS = 12
HD = 128
TOK_DEV = 64
HOLDERS = 16
MICRO = 2
SEQS = 1
TOKENS = 1024


def rough_part(base_key, salt_value):
    use_key = jax.random.fold_in(base_key, salt_value)
    return jnp.clip(1.5 * jax.random.normal(use_key, (MICRO, TOKENS, HEADS * HD), jnp.float32), -6.0, 6.0)


def draw_queries(key, part):
    drawn = rough_part(key, 1)
    return drawn.astype(jnp.bfloat16)


def draw_key_value(key, part):
    keys_part = rough_part(key, 2)
    values_part = jnp.clip(jax.random.normal(jax.random.fold_in(key, 3), (MICRO, TOKENS, HEADS * HD), jnp.float32), -6.0, 6.0)
    return jnp.stack([keys_part, values_part]).astype(jnp.bfloat16)


def setup_inputs(seed: int = 0) -> dict:
    streams_of = jax.random.split(jax.random.key(seed), 3)
    queries = draw_queries(jax.random.fold_in(streams_of[2], 71), 0)
    key_value = draw_key_value(jax.random.fold_in(streams_of[2], 71), 0)
    return dict(queries=queries, key_value=key_value)


def attend_group(group_data):
    query_part, key_part, value_part = group_data
    query_heads = query_part.astype(jnp.float32).reshape(-1, HEADS, HD)
    key_heads = key_part.astype(jnp.float32).reshape(-1, HEADS, HD)
    value_heads = value_part.astype(jnp.float32).reshape(-1, HEADS, HD)
    scores = jnp.einsum("qhd,khd->qhk", query_heads, key_heads) * (HD ** -0.5)
    top_score = jnp.max(scores, axis=-1, keepdims=True)
    weights = jnp.exp(scores - top_score)
    weight_sum = jnp.sum(weights, axis=-1)
    rounded = lax.optimization_barrier(weights.astype(jnp.bfloat16)).astype(jnp.float32)
    attended = jnp.einsum("qhk,khd->qhd", rounded, value_heads) / weight_sum[..., None]
    return attended.reshape(-1, HEADS * HD).astype(jnp.bfloat16)


def regroup(array_in):
    shaped = array_in.reshape(MICRO, HOLDERS, SEQS, TOK_DEV, HEADS * HD)
    shaped = jnp.transpose(shaped, (0, 2, 1, 3, 4))
    return shaped.reshape(MICRO * SEQS, HOLDERS * TOK_DEV, HEADS * HD)


def reference(queries, key_value):
    attended = lax.map(attend_group, (regroup(queries), regroup(key_value[0]), regroup(key_value[1])))
    attended = attended.reshape(MICRO, SEQS, HOLDERS, TOK_DEV, HEADS * HD)
    attended = jnp.transpose(attended, (0, 2, 1, 3, 4)).reshape(MICRO, TOKENS, HEADS * HD)
    return jnp.roll(attended, 1, axis=0)
```

```python
import functools

import jax
import jax.numpy as jnp
from jax import lax
from jax.experimental import pallas as pl
from jax.experimental.pallas import tpu as pltpu
from jax.sharding import PartitionSpec as P

HD = 128
ANY = pl.BlockSpec(memory_space=pl.ANY)
VMEM = pl.BlockSpec(memory_space=pltpu.VMEM)


def group_count(heads, places):
    count = 1
    while heads % (2 * count) == 0 and places % (2 * count) == 0:
        count *= 2
    return count


def split_heads(queries, key_value, groups, inner):
    rows, full = queries.shape[1:]
    width = full // groups

    def kernel(q_ref, kv_ref, *rest):
        outs, sem = rest[:-1], rest[-1]
        mine = lax.axis_index("seq") // inner
        copies = []
        for which in range(3):
            source = q_ref.at[0] if which == 2 else kv_ref.at[which, 0]
            for step in range(groups):
                start = pl.multiple_of((mine ^ step) * width, 128)
                copies.append(
                    pltpu.make_async_copy(
                        source.at[:, pl.ds(start, width)],
                        outs[which * groups + step],
                        sem.at[which * groups + step],
                    )
                )
        for copy in copies:
            copy.start()
        for copy in copies:
            copy.wait()

    pieces = pl.pallas_call(
        kernel,
        out_shape=[jax.ShapeDtypeStruct((rows, width), queries.dtype)] * (3 * groups),
        in_specs=[ANY, ANY],
        out_specs=[VMEM] * (3 * groups),
        scratch_shapes=[pltpu.SemaphoreType.DMA((3 * groups,))],
        name="split_heads",
    )(queries, key_value)
    return pieces[:groups], pieces[groups : 2 * groups], pieces[2 * groups :]


def attend(query_pieces, key_blocks, value_blocks):
    groups = len(query_pieces)
    blocks = len(key_blocks)
    rows, width = query_pieces[0].shape
    contract = (((1,), (1,)), ((), ()))

    def kernel(*refs):
        q_refs = refs[:groups]
        k_refs = refs[groups : groups + blocks]
        v_refs = refs[groups + blocks : groups + 2 * blocks]
        out_refs = refs[groups + 2 * blocks :]
        for head in range(width // HD):
            cols = slice(head * HD, (head + 1) * HD)
            q = jnp.concatenate([ref[:, cols] for ref in q_refs], axis=0)
            scores = [
                lax.dot_general(
                    q, ref[:, cols], contract, preferred_element_type=jnp.float32
                )
                * HD ** (-0.5)
                for ref in k_refs
            ]
            top = functools.reduce(
                jnp.maximum, [jnp.max(s, axis=1, keepdims=True) for s in scores]
            )
            total = 0.0
            acc = 0.0
            for s, ref in zip(scores, v_refs):
                weights = jnp.exp(s - top)
                total = total + jnp.sum(weights, axis=1, keepdims=True)
                acc = acc + jnp.dot(
                    weights.astype(jnp.bfloat16),
                    ref[:, cols],
                    preferred_element_type=jnp.float32,
                )
            out = (acc / total).astype(jnp.bfloat16)
            for step, ref in enumerate(out_refs):
                ref[:, cols] = out[step * rows : (step + 1) * rows]

    return pl.pallas_call(
        kernel,
        out_shape=[jax.ShapeDtypeStruct((rows, width), jnp.bfloat16)] * groups,
        in_specs=[VMEM] * (groups + 2 * blocks),
        out_specs=[VMEM] * groups,
        name="attend",
    )(*query_pieces, *key_blocks, *value_blocks)


def join_heads(pieces, inner):
    groups = len(pieces)
    rows, width = pieces[0].shape

    def kernel(*refs):
        out_ref, sem = refs[groups:]
        mine = lax.axis_index("seq") // inner
        copies = [
            pltpu.make_async_copy(
                refs[step],
                out_ref.at[0, :, pl.ds(pl.multiple_of((mine ^ step) * width, 128), width)],
                sem.at[step],
            )
            for step in range(groups)
        ]
        for copy in copies:
            copy.start()
        for copy in copies:
            copy.wait()

    return pl.pallas_call(
        kernel,
        out_shape=jax.ShapeDtypeStruct((1, rows, groups * width), jnp.bfloat16),
        in_specs=[VMEM] * groups,
        out_specs=ANY,
        scratch_shapes=[pltpu.SemaphoreType.DMA((groups,))],
        name="join_heads",
    )(*pieces)


def shards(queries, key_value):
    places = lax.axis_size("seq")
    segments = lax.axis_size("segment")
    heads = queries.shape[2] // HD
    groups = group_count(heads, places)
    inner = places // groups

    def swap(value, bits):
        return lax.ppermute(value, "seq", [(i, i ^ bits) for i in range(places)])

    def exchange(pieces):
        far = [swap(pieces[s], s * inner) for s in range(groups - 1, 0, -1)]
        return [pieces[0]] + far[::-1]

    def gather(pieces):
        blocks = [jnp.concatenate(exchange(pieces), axis=0)]
        bits = inner // 2
        while bits:
            blocks = blocks + [swap(block, bits) for block in blocks]
            bits //= 2
        return blocks

    keys, values, query_pieces = split_heads(queries, key_value, groups, inner)
    key_blocks = gather(keys)
    value_blocks = gather(values)
    query_pieces = exchange(query_pieces)
    attended = attend(query_pieces, key_blocks, value_blocks)

    def hand(value, step):
        pairs = [
            (
                segment * places + i,
                ((segment + 1) % segments) * places + (i ^ (step * inner)),
            )
            for segment in range(segments)
            for i in range(places)
        ]
        return lax.ppermute(value, ("segment", "seq"), pairs)

    handed = [hand(attended[s], s) for s in range(groups - 1, -1, -1)][::-1]
    return join_heads(handed, inner)


def solution(mesh):
    return jax.shard_map(
        shards,
        mesh=mesh,
        in_specs=(P("segment", "seq", None), P(None, "segment", "seq", None)),
        out_specs=P("segment", "seq", None),
        check_vma=False,
    )
```

```python
import jax
import jax.numpy as jnp
from jax import lax
from jax.experimental import pallas as pl
from jax.experimental.pallas import tpu as pltpu
from jax.sharding import PartitionSpec as P

HD = 128
HBM = pl.BlockSpec(memory_space=pltpu.HBM)
VMEM = pl.BlockSpec(memory_space=pltpu.VMEM)
PARAMS = pltpu.CompilerParams(vmem_limit_bytes=16 << 20)


def group_count(heads, places):
    count = 1
    while heads % (2 * count) == 0 and places % (2 * count) == 0:
        count *= 2
    return count


def run_copies(pairs, sem):
    copies = [
        pltpu.make_async_copy(source, target, sem.at[i])
        for i, (source, target) in enumerate(pairs)
    ]
    for copy in copies:
        copy.start()
    for copy in copies:
        copy.wait()


def group_columns(step, inner, width):
    mine = lax.axis_index("seq") // inner
    return pl.ds(pl.multiple_of((mine ^ step) * width, HD), width)


def split_heads(queries, key_value, groups, inner):
    rows, full = queries.shape[1:]
    width = full // groups

    def kernel(q_ref, kv_ref, *rest):
        first, second, sem = rest[:groups], rest[groups : 2 * groups], rest[-1]
        mine = lax.axis_index("seq") // inner
        pairs = []
        for step in range(groups):
            start = (mine ^ step) * width
            cols = pl.ds(pl.multiple_of(start, HD), width)
            pairs.append((kv_ref.at[0, 0, :, cols], first[step]))
            pairs.append((kv_ref.at[1, 0, :, cols], second[step].at[:, pl.ds(0, width)]))
            pairs.append((q_ref.at[0, :, cols], second[step].at[:, pl.ds(width, width)]))
        run_copies(pairs, sem)

    out = pl.pallas_call(
        kernel,
        out_shape=[jax.ShapeDtypeStruct((rows, width), queries.dtype)] * groups
        + [jax.ShapeDtypeStruct((rows, 2 * width), queries.dtype)] * groups,
        in_specs=[HBM, HBM],
        out_specs=[VMEM] * (2 * groups),
        scratch_shapes=[pltpu.SemaphoreType.DMA((3 * groups,))],
        name="split_heads",
        compiler_params=PARAMS,
    )(
        pltpu.with_memory_space_constraint(queries, pltpu.HBM),
        pltpu.with_memory_space_constraint(key_value, pltpu.HBM),
    )
    return out[:groups], out[groups:]


def weigh(query_pieces, key_blocks, width):
    groups, blocks = len(query_pieces), len(key_blocks)
    rows = query_pieces[0].shape[0]
    offset = query_pieces[0].shape[1] - width
    heads, keys = width // HD, sum(block.shape[0] for block in key_blocks)
    contract = (((1,), (1,)), ((), ()))

    def kernel(*refs):
        query_refs, key_refs = refs[:groups], refs[groups : groups + blocks]
        weights_ref, sums_ref = refs[groups + blocks :]
        for head in range(heads):
            cols = slice(head * HD, (head + 1) * HD)
            q_cols = slice(offset + head * HD, offset + (head + 1) * HD)
            q = jnp.concatenate([ref[:, q_cols] for ref in query_refs], axis=0)
            k = jnp.concatenate([ref[:, cols] for ref in key_refs], axis=0)
            scores = lax.dot_general(q, k, contract, preferred_element_type=jnp.float32)
            scores = scores * HD ** (-0.5)
            weights = jnp.exp(scores - jnp.max(scores, axis=1, keepdims=True))
            sums_ref[:, head : head + 1] = jnp.sum(weights, axis=1, keepdims=True)
            weights_ref[head] = weights.astype(jnp.bfloat16)

    return pl.pallas_call(
        kernel,
        out_shape=[
            jax.ShapeDtypeStruct((heads, groups * rows, keys), jnp.bfloat16),
            jax.ShapeDtypeStruct((groups * rows, HD), jnp.float32),
        ],
        in_specs=[VMEM] * (groups + blocks),
        out_specs=[VMEM] * 2,
        name="weigh",
        compiler_params=PARAMS,
    )(*query_pieces, *key_blocks)


def average(weights, sums, value_blocks, groups):
    heads, queries, keys = weights.shape
    rows = queries // groups
    blocks = len(value_blocks)

    def kernel(weights_ref, sums_ref, *refs):
        value_refs, out_refs = refs[:blocks], refs[blocks:]
        for head in range(heads):
            cols = slice(head * HD, (head + 1) * HD)
            v = jnp.concatenate([ref[:, cols] for ref in value_refs], axis=0)
            total = jnp.dot(weights_ref[head], v, preferred_element_type=jnp.float32)
            out = (total / sums_ref[:, head : head + 1]).astype(jnp.bfloat16)
            for step, ref in enumerate(out_refs):
                ref[:, cols] = out[step * rows : (step + 1) * rows]

    return pl.pallas_call(
        kernel,
        out_shape=[jax.ShapeDtypeStruct((rows, heads * HD), jnp.bfloat16)] * groups,
        in_specs=[VMEM] * (2 + blocks),
        out_specs=[VMEM] * groups,
        name="average",
        compiler_params=PARAMS,
    )(weights, sums, *value_blocks)


def join_heads(pieces, inner):
    groups = len(pieces)
    rows, width = pieces[0].shape

    def kernel(*refs):
        out_ref, sem = refs[groups:]
        run_copies(
            [
                (refs[step], out_ref.at[0, :, group_columns(step, inner, width)])
                for step in range(groups)
            ],
            sem,
        )

    return pl.pallas_call(
        kernel,
        out_shape=jax.ShapeDtypeStruct((1, rows, groups * width), jnp.bfloat16),
        in_specs=[VMEM] * groups,
        out_specs=pl.BlockSpec(memory_space=pl.ANY),
        scratch_shapes=[pltpu.SemaphoreType.DMA((groups,))],
        name="join_heads",
        compiler_params=PARAMS,
    )(*pieces)


def shards(queries, key_value):
    places = lax.axis_size("seq")
    segments = lax.axis_size("segment")
    rows = queries.shape[1]
    groups = group_count(queries.shape[2] // HD, places)
    inner = places // groups

    def swap(value, bits):
        return lax.ppermute(value, "seq", [(i, i ^ bits) for i in range(places)])

    def exchange(pieces):
        far = [swap(pieces[s], s * inner) for s in range(groups - 1, 0, -1)]
        return [pieces[0]] + far[::-1]

    def gather(block):
        blocks, bits = [block], inner // 2
        while bits:
            blocks = blocks + [swap(block, bits) for block in blocks]
            bits //= 2
        return blocks

    width = queries.shape[2] // groups
    first, second = split_heads(queries, key_value, groups, inner)
    first, second = exchange(first), exchange(second)
    key_blocks = gather(jnp.concatenate(first, axis=0))
    value_blocks = gather(jnp.concatenate([piece[:, :width] for piece in second], axis=0))
    weights, sums = weigh(second, key_blocks, width)
    attended = average(weights, sums, value_blocks, groups)

    def hand(value, step):
        pairs = [
            (
                segment * places + i,
                ((segment + 1) % segments) * places + (i ^ (step * inner)),
            )
            for segment in range(segments)
            for i in range(places)
        ]
        return lax.ppermute(value, ("segment", "seq"), pairs)

    handed = [hand(attended[s], s) for s in range(groups - 1, -1, -1)][::-1]
    return join_heads(handed, inner)


def solution(mesh):
    return jax.shard_map(
        shards,
        mesh=mesh,
        in_specs=(P("segment", "seq", None), P(None, "segment", "seq", None)),
        out_specs=P("segment", "seq", None),
        check_vma=False,
    )
```

```python
import jax
import jax.numpy as jnp
from jax import lax
from jax.experimental import pallas as pl
from jax.experimental.pallas import tpu as pltpu
from jax.sharding import PartitionSpec as P

HD = 128
HBM = pl.BlockSpec(memory_space=pltpu.HBM)
VMEM = pl.BlockSpec(memory_space=pltpu.VMEM)
PARAMS = pltpu.CompilerParams(vmem_limit_bytes=16 << 20)


def group_count(heads, places):
    count = 1
    while heads % (2 * count) == 0 and places % (2 * count) == 0:
        count *= 2
    return count


def run_copies(pairs, sem):
    copies = [
        pltpu.make_async_copy(source, target, sem.at[i])
        for i, (source, target) in enumerate(pairs)
    ]
    for copy in copies:
        copy.start()
    for copy in copies:
        copy.wait()


def group_columns(step, inner, width):
    mine = lax.axis_index("seq") // inner
    return pl.ds(pl.multiple_of((mine ^ step) * width, HD), width)


def split_heads(queries, key_value, groups, inner):
    rows, full = queries.shape[1:]
    width = full // groups

    def kernel(q_ref, kv_ref, *rest):
        first, second, sem = rest[:groups], rest[groups : 2 * groups], rest[-1]
        mine = lax.axis_index("seq") // inner
        pairs = []
        for step in range(groups):
            start = (mine ^ step) * width
            cols = pl.ds(pl.multiple_of(start, HD), width)
            pairs.append((kv_ref.at[0, 0, :, cols], first[step]))
            pairs.append((kv_ref.at[1, 0, :, cols], second[step].at[:, pl.ds(0, width)]))
            pairs.append((q_ref.at[0, :, cols], second[step].at[:, pl.ds(width, width)]))
        run_copies(pairs, sem)

    out = pl.pallas_call(
        kernel,
        out_shape=[jax.ShapeDtypeStruct((rows, width), queries.dtype)] * groups
        + [jax.ShapeDtypeStruct((rows, 2 * width), queries.dtype)] * groups,
        in_specs=[HBM, HBM],
        out_specs=[VMEM] * (2 * groups),
        scratch_shapes=[pltpu.SemaphoreType.DMA((3 * groups,))],
        name="split_heads",
        compiler_params=PARAMS,
    )(
        pltpu.with_memory_space_constraint(queries, pltpu.HBM),
        pltpu.with_memory_space_constraint(key_value, pltpu.HBM),
    )
    return out[:groups], out[groups:]


def weigh(query_pieces, key_blocks, width):
    groups, blocks = len(query_pieces), len(key_blocks)
    rows = query_pieces[0].shape[0]
    offset = query_pieces[0].shape[1] - width
    heads, keys = width // HD, sum(block.shape[0] for block in key_blocks)
    contract = (((1,), (1,)), ((), ()))

    def kernel(*refs):
        query_refs, key_refs = refs[:groups], refs[groups : groups + blocks]
        weights_ref, sums_ref = refs[groups + blocks :]
        for head in range(heads):
            cols = slice(head * HD, (head + 1) * HD)
            q_cols = slice(offset + head * HD, offset + (head + 1) * HD)
            q = jnp.concatenate([ref[:, q_cols] for ref in query_refs], axis=0)
            k = jnp.concatenate([ref[:, cols] for ref in key_refs], axis=0)
            scores = lax.dot_general(q, k, contract, preferred_element_type=jnp.float32)
            scores = scores * HD ** (-0.5)
            weights = jnp.exp(scores - jnp.max(scores, axis=1, keepdims=True))
            sums_ref[:, head : head + 1] = jnp.sum(weights, axis=1, keepdims=True)
            weights_ref[head] = weights.astype(jnp.bfloat16)

    return pl.pallas_call(
        kernel,
        out_shape=[
            jax.ShapeDtypeStruct((heads, groups * rows, keys), jnp.bfloat16),
            jax.ShapeDtypeStruct((groups * rows, HD), jnp.float32),
        ],
        in_specs=[VMEM] * (groups + blocks),
        out_specs=[VMEM] * 2,
        name="weigh",
        compiler_params=PARAMS,
    )(*query_pieces, *key_blocks)


def average(weights, sums, value_blocks, groups):
    heads, queries, keys = weights.shape
    rows = queries // groups
    blocks = len(value_blocks)

    def kernel(weights_ref, sums_ref, *refs):
        value_refs, out_refs = refs[:blocks], refs[blocks:]
        for head in range(heads):
            cols = slice(head * HD, (head + 1) * HD)
            v = jnp.concatenate([ref[:, cols] for ref in value_refs], axis=0)
            total = jnp.dot(weights_ref[head], v, preferred_element_type=jnp.float32)
            out = (total / sums_ref[:, head : head + 1]).astype(jnp.bfloat16)
            for step, ref in enumerate(out_refs):
                ref[:, cols] = out[step * rows : (step + 1) * rows]

    return pl.pallas_call(
        kernel,
        out_shape=[jax.ShapeDtypeStruct((rows, heads * HD), jnp.bfloat16)] * groups,
        in_specs=[VMEM] * (2 + blocks),
        out_specs=[VMEM] * groups,
        name="average",
        compiler_params=PARAMS,
    )(weights, sums, *value_blocks)


def join_heads(pieces, inner):
    groups = len(pieces)
    rows, width = pieces[0].shape

    def kernel(*refs):
        out_ref, sem = refs[groups:]
        run_copies(
            [
                (refs[step], out_ref.at[0, :, group_columns(step, inner, width)])
                for step in range(groups)
            ],
            sem,
        )

    return pl.pallas_call(
        kernel,
        out_shape=jax.ShapeDtypeStruct((1, rows, groups * width), jnp.bfloat16),
        in_specs=[VMEM] * groups,
        out_specs=pl.BlockSpec(memory_space=pl.ANY),
        scratch_shapes=[pltpu.SemaphoreType.DMA((groups,))],
        name="join_heads",
        compiler_params=PARAMS,
    )(*pieces)


def shards(queries, key_value):
    places = lax.axis_size("seq")
    segments = lax.axis_size("segment")
    rows = queries.shape[1]
    groups = group_count(queries.shape[2] // HD, places)
    inner = places // groups

    def swap(value, bits):
        return lax.ppermute(value, "seq", [(i, i ^ bits) for i in range(places)])

    def exchange(pieces):
        far = [swap(pieces[s], s * inner) for s in range(groups - 1, 0, -1)]
        return [pieces[0]] + far[::-1]

    def gather(parts):
        blocks, bits = list(parts), inner // 2
        while bits > 1:
            blocks = blocks + [swap(block, bits) for block in blocks]
            bits //= 2
        return blocks

    def with_other_core(blocks):
        return blocks + [swap(block, 1) for block in blocks] if inner > 1 else blocks

    width = queries.shape[2] // groups
    first, second = split_heads(queries, key_value, groups, inner)
    first, second = exchange(first), exchange(second)
    key_blocks = with_other_core(
        [jnp.concatenate(gather([jnp.concatenate(first, axis=0)]), axis=0)]
    )
    values = [piece[:, :width] for piece in second]
    near, far = values[: groups // 2], values[groups // 2 :]
    parts = [jnp.concatenate(some, axis=0) for some in (near, far) if some]
    blocks = gather(parts)
    count = len(parts)
    value_blocks = with_other_core(
        [
            jnp.concatenate(blocks[i : i + count], axis=0)
            for i in range(0, len(blocks), count)
        ]
    )
    weights, sums = weigh(second, key_blocks, width)
    attended = average(weights, sums, value_blocks, groups)

    def hand(value, step):
        pairs = [
            (
                segment * places + i,
                ((segment + 1) % segments) * places + (i ^ (step * inner)),
            )
            for segment in range(segments)
            for i in range(places)
        ]
        return lax.ppermute(value, ("segment", "seq"), pairs)

    handed = [hand(attended[s], s) for s in range(groups)]
    return join_heads(handed, inner)


def solution(mesh):
    return jax.shard_map(
        shards,
        mesh=mesh,
        in_specs=(P("segment", "seq", None), P(None, "segment", "seq", None)),
        out_specs=P("segment", "seq", None),
        check_vma=False,
    )
```

```python
import jax
import jax.numpy as jnp
from jax import lax
from jax.experimental import pallas as pl
from jax.experimental.pallas import tpu as pltpu
from jax.sharding import PartitionSpec as P

HD = 128
HBM = pl.BlockSpec(memory_space=pltpu.HBM)
VMEM = pl.BlockSpec(memory_space=pltpu.VMEM)
PARAMS = pltpu.CompilerParams(vmem_limit_bytes=16 << 20)


def group_count(heads, places):
    count = 1
    while heads % (2 * count) == 0 and places % (2 * count) == 0:
        count *= 2
    return count


def run_copies(pairs, sem):
    copies = [
        pltpu.make_async_copy(source, target, sem.at[i])
        for i, (source, target) in enumerate(pairs)
    ]
    for copy in copies:
        copy.start()
    for copy in copies:
        copy.wait()


def group_columns(step, inner, width):
    mine = lax.axis_index("seq") // inner
    return pl.ds(pl.multiple_of((mine ^ step) * width, HD), width)


def split_heads(queries, key_value, groups, inner):
    rows, full = queries.shape[1:]
    width = full // groups

    def kernel(q_ref, kv_ref, *rest):
        first, second, sem = rest[:groups], rest[groups : 2 * groups], rest[-1]
        mine = lax.axis_index("seq") // inner
        pairs = []
        for step in range(groups):
            start = (mine ^ step) * width
            cols = pl.ds(pl.multiple_of(start, HD), width)
            pairs.append((kv_ref.at[0, 0, :, cols], first[step]))
            pairs.append((kv_ref.at[1, 0, :, cols], second[step].at[:, pl.ds(0, width)]))
            pairs.append((q_ref.at[0, :, cols], second[step].at[:, pl.ds(width, width)]))
        run_copies(pairs, sem)

    out = pl.pallas_call(
        kernel,
        out_shape=[jax.ShapeDtypeStruct((rows, width), queries.dtype)] * groups
        + [jax.ShapeDtypeStruct((rows, 2 * width), queries.dtype)] * groups,
        in_specs=[HBM, HBM],
        out_specs=[VMEM] * (2 * groups),
        scratch_shapes=[pltpu.SemaphoreType.DMA((3 * groups,))],
        name="split_heads",
        compiler_params=PARAMS,
    )(
        pltpu.with_memory_space_constraint(queries, pltpu.HBM),
        pltpu.with_memory_space_constraint(key_value, pltpu.HBM),
    )
    return out[:groups], out[groups:]


def weigh(query_pieces, key_blocks, width):
    groups, blocks = len(query_pieces), len(key_blocks)
    rows = query_pieces[0].shape[0]
    offset = query_pieces[0].shape[1] - width
    heads, keys = width // HD, sum(block.shape[0] for block in key_blocks)
    contract = (((1,), (1,)), ((), ()))

    def kernel(*refs):
        query_refs, key_refs = refs[:groups], refs[groups : groups + blocks]
        weights_ref, sums_ref = refs[groups + blocks :]
        for head in range(heads):
            cols = slice(head * HD, (head + 1) * HD)
            q_cols = slice(offset + head * HD, offset + (head + 1) * HD)
            q = jnp.concatenate([ref[:, q_cols] for ref in query_refs], axis=0)
            k = jnp.concatenate([ref[:, cols] for ref in key_refs], axis=0)
            scores = lax.dot_general(q, k, contract, preferred_element_type=jnp.float32)
            scores = scores * HD ** (-0.5)
            weights = jnp.exp(scores - jnp.max(scores, axis=1, keepdims=True))
            sums_ref[:, head : head + 1] = jnp.sum(weights, axis=1, keepdims=True)
            weights_ref[head] = weights.astype(jnp.bfloat16)

    return pl.pallas_call(
        kernel,
        out_shape=[
            jax.ShapeDtypeStruct((heads, groups * rows, keys), jnp.bfloat16),
            jax.ShapeDtypeStruct((groups * rows, HD), jnp.float32),
        ],
        in_specs=[VMEM] * (groups + blocks),
        out_specs=[VMEM] * 2,
        name="weigh",
        compiler_params=PARAMS,
    )(*query_pieces, *key_blocks)


def average(weights, sums, value_blocks, groups, first, last, after):
    heads, queries, keys = weights.shape
    rows = queries // groups
    blocks = len(value_blocks)

    def kernel(weights_ref, sums_ref, *refs):
        value_refs, out_refs = refs[:blocks], refs[blocks + len(after) :]
        some = slice(first * rows, last * rows)
        for head in range(heads):
            cols = slice(head * HD, (head + 1) * HD)
            v = jnp.concatenate([ref[:, cols] for ref in value_refs], axis=0)
            total = jnp.dot(weights_ref[head, some], v, preferred_element_type=jnp.float32)
            out = (total / sums_ref[some, head : head + 1]).astype(jnp.bfloat16)
            for step, ref in enumerate(out_refs):
                ref[:, cols] = out[step * rows : (step + 1) * rows]

    return pl.pallas_call(
        kernel,
        out_shape=[jax.ShapeDtypeStruct((rows, heads * HD), jnp.bfloat16)] * (last - first),
        in_specs=[VMEM] * (2 + blocks) + [pl.BlockSpec(memory_space=pl.ANY)] * len(after),
        out_specs=[VMEM] * (last - first),
        name="average",
        compiler_params=PARAMS,
    )(weights, sums, *value_blocks, *after)


def join_heads(pieces, inner):
    groups = len(pieces)
    rows, width = pieces[0].shape

    def kernel(*refs):
        out_ref, sem = refs[groups:]
        run_copies(
            [
                (refs[step], out_ref.at[0, :, group_columns(step, inner, width)])
                for step in range(groups)
            ],
            sem,
        )

    return pl.pallas_call(
        kernel,
        out_shape=jax.ShapeDtypeStruct((1, rows, groups * width), jnp.bfloat16),
        in_specs=[VMEM] * groups,
        out_specs=pl.BlockSpec(memory_space=pl.ANY),
        scratch_shapes=[pltpu.SemaphoreType.DMA((groups,))],
        name="join_heads",
        compiler_params=PARAMS,
    )(*pieces)


def shards(queries, key_value):
    places = lax.axis_size("seq")
    segments = lax.axis_size("segment")
    rows = queries.shape[1]
    groups = group_count(queries.shape[2] // HD, places)
    inner = places // groups

    def swap(value, bits):
        return lax.ppermute(value, "seq", [(i, i ^ bits) for i in range(places)])

    def exchange(pieces):
        far = [swap(pieces[s], s * inner) for s in range(groups - 1, 0, -1)]
        return [pieces[0]] + far[::-1]

    def gather(parts):
        blocks, bits = list(parts), inner // 2
        while bits > 1:
            blocks = blocks + [swap(block, bits) for block in blocks]
            bits //= 2
        return blocks

    def with_other_core(blocks):
        return blocks + [swap(block, 1) for block in blocks] if inner > 1 else blocks

    width = queries.shape[2] // groups
    first, second = split_heads(queries, key_value, groups, inner)
    first, second = exchange(first), exchange(second)
    key_blocks = with_other_core(
        [jnp.concatenate(gather([jnp.concatenate(first, axis=0)]), axis=0)]
    )
    values = [piece[:, :width] for piece in second]
    near, far = values[: groups // 2], values[groups // 2 :]
    parts = [jnp.concatenate(some, axis=0) for some in (near, far) if some]
    blocks = gather(parts)
    count = len(parts)
    value_blocks = with_other_core(
        [
            jnp.concatenate(blocks[i : i + count], axis=0)
            for i in range(0, len(blocks), count)
        ]
    )
    weights, sums = weigh(second, key_blocks, width)
    own = average(weights, sums, value_blocks, groups, 0, 1, [])
    attended = own + average(weights, sums, value_blocks, groups, 1, groups, own)

    def hand(value, step):
        pairs = [
            (
                segment * places + i,
                ((segment + 1) % segments) * places + (i ^ (step * inner)),
            )
            for segment in range(segments)
            for i in range(places)
        ]
        return lax.ppermute(value, ("segment", "seq"), pairs)

    handed = [hand(attended[s], s) for s in range(groups)]
    return join_heads(handed, inner)


def solution(mesh):
    return jax.shard_map(
        shards,
        mesh=mesh,
        in_specs=(P("segment", "seq", None), P(None, "segment", "seq", None)),
        out_specs=P("segment", "seq", None),
        check_vma=False,
    )
```

```python
import jax
import jax.numpy as jnp
from jax import lax
from jax.experimental import pallas as pl
from jax.experimental.pallas import tpu as pltpu
from jax.sharding import PartitionSpec as P

HD = 128
LOG2_E = 1.4426950408889634
HBM = pl.BlockSpec(memory_space=pltpu.HBM)
VMEM = pl.BlockSpec(memory_space=pltpu.VMEM)
PARAMS = pltpu.CompilerParams(vmem_limit_bytes=16 << 20)


def group_count(heads, places):
    count = 1
    while heads % (2 * count) == 0 and places % (2 * count) == 0:
        count *= 2
    return count


def run_copies(pairs, sem):
    copies = [
        pltpu.make_async_copy(source, target, sem.at[i])
        for i, (source, target) in enumerate(pairs)
    ]
    for copy in copies:
        copy.start()
    for copy in copies:
        copy.wait()


def group_columns(step, inner, width):
    mine = lax.axis_index("seq") // inner
    return pl.ds(pl.multiple_of((mine ^ step) * width, HD), width)


def split_heads(queries, key_value, groups, inner):
    rows, full = queries.shape[1:]
    width = full // groups

    def kernel(q_ref, kv_ref, *rest):
        first, second, sem = rest[:groups], rest[groups : 2 * groups], rest[-1]
        mine = lax.axis_index("seq") // inner
        pairs = []
        for step in range(groups):
            start = (mine ^ step) * width
            cols = pl.ds(pl.multiple_of(start, HD), width)
            pairs.append((kv_ref.at[0, 0, :, cols], first[step]))
            pairs.append((kv_ref.at[1, 0, :, cols], second[step].at[:, pl.ds(0, width)]))
            pairs.append((q_ref.at[0, :, cols], second[step].at[:, pl.ds(width, width)]))
        run_copies(pairs, sem)

    out = pl.pallas_call(
        kernel,
        out_shape=[jax.ShapeDtypeStruct((rows, width), queries.dtype)] * groups
        + [jax.ShapeDtypeStruct((rows, 2 * width), queries.dtype)] * groups,
        in_specs=[HBM, HBM],
        out_specs=[VMEM] * (2 * groups),
        scratch_shapes=[pltpu.SemaphoreType.DMA((3 * groups,))],
        name="split_heads",
        compiler_params=PARAMS,
    )(
        pltpu.with_memory_space_constraint(queries, pltpu.HBM),
        pltpu.with_memory_space_constraint(key_value, pltpu.HBM),
    )
    return out[:groups], out[groups:]


def weigh(query_pieces, key_blocks, width):
    groups, blocks = len(query_pieces), len(key_blocks)
    rows = query_pieces[0].shape[0]
    offset = query_pieces[0].shape[1] - width
    heads, keys = width // HD, sum(block.shape[0] for block in key_blocks)
    contract = (((1,), (1,)), ((), ()))

    def kernel(*refs):
        query_refs, key_refs = refs[:groups], refs[groups : groups + blocks]
        weights_ref, sums_ref = refs[groups + blocks :]
        for head in range(heads):
            cols = slice(head * HD, (head + 1) * HD)
            q_cols = slice(offset + head * HD, offset + (head + 1) * HD)
            q = jnp.concatenate([ref[:, q_cols] for ref in query_refs], axis=0)
            k = jnp.concatenate([ref[:, cols] for ref in key_refs], axis=0)
            scores = lax.dot_general(q, k, contract, preferred_element_type=jnp.float32)
            scores = scores * (HD ** (-0.5) * LOG2_E)
            weights = jnp.exp2(scores - jnp.max(scores, axis=1, keepdims=True))
            sums_ref[:, head : head + 1] = jnp.sum(weights, axis=1, keepdims=True)
            weights_ref[head] = weights.astype(jnp.bfloat16)

    return pl.pallas_call(
        kernel,
        out_shape=[
            jax.ShapeDtypeStruct((heads, groups * rows, keys), jnp.bfloat16),
            jax.ShapeDtypeStruct((groups * rows, HD), jnp.float32),
        ],
        in_specs=[VMEM] * (groups + blocks),
        out_specs=[VMEM] * 2,
        name="weigh",
        compiler_params=PARAMS,
    )(*query_pieces, *key_blocks)


def average(weights, sums, value_blocks, groups, first, last, after):
    heads, queries, keys = weights.shape
    rows = queries // groups
    blocks = len(value_blocks)

    def kernel(weights_ref, sums_ref, *refs):
        value_refs, out_refs = refs[:blocks], refs[blocks + len(after) :]
        some = slice(first * rows, last * rows)
        for head in range(heads):
            cols = slice(head * HD, (head + 1) * HD)
            v = jnp.concatenate([ref[:, cols] for ref in value_refs], axis=0)
            total = jnp.dot(weights_ref[head, some], v, preferred_element_type=jnp.float32)
            out = (total / sums_ref[some, head : head + 1]).astype(jnp.bfloat16)
            for step, ref in enumerate(out_refs):
                ref[:, cols] = out[step * rows : (step + 1) * rows]

    return pl.pallas_call(
        kernel,
        out_shape=[jax.ShapeDtypeStruct((rows, heads * HD), jnp.bfloat16)] * (last - first),
        in_specs=[VMEM] * (2 + blocks) + [pl.BlockSpec(memory_space=pl.ANY)] * len(after),
        out_specs=[VMEM] * (last - first),
        name="average",
        compiler_params=PARAMS,
    )(weights, sums, *value_blocks, *after)


def join_heads(pieces, inner):
    groups = len(pieces)
    rows, width = pieces[0].shape

    def kernel(*refs):
        out_ref, sem = refs[groups:]
        run_copies(
            [
                (refs[step], out_ref.at[0, :, group_columns(step, inner, width)])
                for step in range(groups)
            ],
            sem,
        )

    return pl.pallas_call(
        kernel,
        out_shape=jax.ShapeDtypeStruct((1, rows, groups * width), jnp.bfloat16),
        in_specs=[VMEM] * groups,
        out_specs=pl.BlockSpec(memory_space=pl.ANY),
        scratch_shapes=[pltpu.SemaphoreType.DMA((groups,))],
        name="join_heads",
        compiler_params=PARAMS,
    )(*pieces)


def shards(queries, key_value):
    places = lax.axis_size("seq")
    segments = lax.axis_size("segment")
    rows = queries.shape[1]
    groups = group_count(queries.shape[2] // HD, places)
    inner = places // groups

    def swap(value, bits):
        return lax.ppermute(value, "seq", [(i, i ^ bits) for i in range(places)])

    def exchange(pieces):
        far = [swap(pieces[s], s * inner) for s in range(groups - 1, 0, -1)]
        return [pieces[0]] + far[::-1]

    def gather(parts):
        blocks, bits = list(parts), inner // 2
        while bits > 1:
            blocks = blocks + [swap(block, bits) for block in blocks]
            bits //= 2
        return blocks

    def with_other_core(blocks):
        return blocks + [swap(block, 1) for block in blocks] if inner > 1 else blocks

    width = queries.shape[2] // groups
    first, second = split_heads(queries, key_value, groups, inner)
    first, second = exchange(first), exchange(second)

    def near_and_far(pieces):
        halves = (pieces[: groups // 2], pieces[groups // 2 :])
        return [jnp.concatenate(some, axis=0) for some in halves if some]

    key_blocks = with_other_core(
        [jnp.concatenate(gather(near_and_far(first)), axis=0)]
    )
    parts = near_and_far([piece[:, :width] for piece in second])
    blocks = gather(parts)
    count = len(parts)
    value_blocks = with_other_core(
        [
            jnp.concatenate(blocks[i : i + count], axis=0)
            for i in range(0, len(blocks), count)
        ]
    )
    weights, sums = weigh(second, key_blocks, width)
    own = average(weights, sums, value_blocks, groups, 0, 1, [])
    attended = own + average(weights, sums, value_blocks, groups, 1, groups, own)

    def hand(value, step):
        pairs = [
            (
                segment * places + i,
                ((segment + 1) % segments) * places + (i ^ (step * inner)),
            )
            for segment in range(segments)
            for i in range(places)
        ]
        return lax.ppermute(value, ("segment", "seq"), pairs)

    handed = [hand(attended[s], s) for s in range(groups)]
    return join_heads(handed, inner)


def solution(mesh):
    return jax.shard_map(
        shards,
        mesh=mesh,
        in_specs=(P("segment", "seq", None), P(None, "segment", "seq", None)),
        out_specs=P("segment", "seq", None),
        check_vma=False,
    )
```

```python
import jax
import jax.numpy as jnp
from jax import lax
from jax.experimental import pallas as pl
from jax.experimental.pallas import tpu as pltpu
from jax.sharding import PartitionSpec as P

HD = 128
LOG2_E = 1.4426950408889634
HBM = pl.BlockSpec(memory_space=pltpu.HBM)
VMEM = pl.BlockSpec(memory_space=pltpu.VMEM)
PARAMS = pltpu.CompilerParams(vmem_limit_bytes=16 << 20)


def group_count(heads, places):
    count = 1
    while heads % (2 * count) == 0 and places % (2 * count) == 0:
        count *= 2
    return count


def run_copies(pairs, sem):
    copies = [
        pltpu.make_async_copy(source, target, sem.at[i])
        for i, (source, target) in enumerate(pairs)
    ]
    for copy in copies:
        copy.start()
    for copy in copies:
        copy.wait()


def group_columns(step, inner, width):
    mine = lax.axis_index("seq") // inner
    return pl.ds(pl.multiple_of((mine ^ step) * width, HD), width)


def split_heads(queries, key_value, groups, inner):
    rows, full = queries.shape[1:]
    width = full // groups

    def kernel(q_ref, kv_ref, *rest):
        first, second, sem = rest[:groups], rest[groups : 2 * groups], rest[-1]
        mine = lax.axis_index("seq") // inner
        pairs = []
        for step in range(groups):
            start = (mine ^ step) * width
            cols = pl.ds(pl.multiple_of(start, HD), width)
            pairs.append((kv_ref.at[0, 0, :, cols], first[step]))
            pairs.append((kv_ref.at[1, 0, :, cols], second[step].at[:, pl.ds(0, width)]))
            pairs.append((q_ref.at[0, :, cols], second[step].at[:, pl.ds(width, width)]))
        run_copies(pairs, sem)

    out = pl.pallas_call(
        kernel,
        out_shape=[jax.ShapeDtypeStruct((rows, width), queries.dtype)] * groups
        + [jax.ShapeDtypeStruct((rows, 2 * width), queries.dtype)] * groups,
        in_specs=[HBM, HBM],
        out_specs=[VMEM] * (2 * groups),
        scratch_shapes=[pltpu.SemaphoreType.DMA((3 * groups,))],
        name="split_heads",
        compiler_params=PARAMS,
    )(
        pltpu.with_memory_space_constraint(queries, pltpu.HBM),
        pltpu.with_memory_space_constraint(key_value, pltpu.HBM),
    )
    return out[:groups], out[groups:]


def weigh(query_pieces, key_blocks, width):
    groups, blocks = len(query_pieces), len(key_blocks)
    rows = query_pieces[0].shape[0]
    offset = query_pieces[0].shape[1] - width
    heads, keys = width // HD, sum(block.shape[0] for block in key_blocks)
    contract = (((1,), (1,)), ((), ()))

    def kernel(*refs):
        query_refs, key_refs = refs[:groups], refs[groups : groups + blocks]
        weights_ref, sums_ref = refs[groups + blocks :]
        for head in range(heads):
            cols = slice(head * HD, (head + 1) * HD)
            q_cols = slice(offset + head * HD, offset + (head + 1) * HD)
            q = jnp.concatenate([ref[:, q_cols] for ref in query_refs], axis=0)
            k = jnp.concatenate([ref[:, cols] for ref in key_refs], axis=0)
            scores = lax.dot_general(q, k, contract, preferred_element_type=jnp.float32)
            scores = scores * (HD ** (-0.5) * LOG2_E)
            weights = jnp.exp2(scores - jnp.max(scores, axis=1, keepdims=True))
            sums_ref[:, head : head + 1] = jnp.sum(weights, axis=1, keepdims=True)
            weights_ref[head] = weights.astype(jnp.bfloat16)

    return pl.pallas_call(
        kernel,
        out_shape=[
            jax.ShapeDtypeStruct((heads, groups * rows, keys), jnp.bfloat16),
            jax.ShapeDtypeStruct((groups * rows, HD), jnp.float32),
        ],
        in_specs=[VMEM] * (groups + blocks),
        out_specs=[VMEM] * 2,
        name="weigh",
        compiler_params=PARAMS,
    )(*query_pieces, *key_blocks)


def average(weights, sums, value_blocks, groups, first, last, after):
    heads, queries, keys = weights.shape
    rows = queries // groups
    blocks = len(value_blocks)

    def kernel(weights_ref, sums_ref, *refs):
        value_refs, out_refs = refs[:blocks], refs[blocks + len(after) :]
        some = slice(first * rows, last * rows)
        for head in range(heads):
            cols = slice(head * HD, (head + 1) * HD)
            v = jnp.concatenate([ref[:, cols] for ref in value_refs], axis=0)
            total = jnp.dot(weights_ref[head, some], v, preferred_element_type=jnp.float32)
            out = (total / sums_ref[some, head : head + 1]).astype(jnp.bfloat16)
            for step, ref in enumerate(out_refs):
                ref[:, cols] = out[step * rows : (step + 1) * rows]

    return pl.pallas_call(
        kernel,
        out_shape=[jax.ShapeDtypeStruct((rows, heads * HD), jnp.bfloat16)] * (last - first),
        in_specs=[VMEM] * (2 + blocks) + [pl.BlockSpec(memory_space=pl.ANY)] * len(after),
        out_specs=[VMEM] * (last - first),
        name="average",
        compiler_params=PARAMS,
    )(weights, sums, *value_blocks, *after)


def join_heads(pieces, inner):
    groups = len(pieces)
    rows, width = pieces[0].shape

    def kernel(*refs):
        out_ref, sem = refs[groups:]
        run_copies(
            [
                (refs[step], out_ref.at[0, :, group_columns(step, inner, width)])
                for step in range(groups)
            ],
            sem,
        )

    return pl.pallas_call(
        kernel,
        out_shape=jax.ShapeDtypeStruct((1, rows, groups * width), jnp.bfloat16),
        in_specs=[VMEM] * groups,
        out_specs=pl.BlockSpec(memory_space=pl.ANY),
        scratch_shapes=[pltpu.SemaphoreType.DMA((groups,))],
        name="join_heads",
        compiler_params=PARAMS,
    )(*pieces)


def shards(queries, key_value):
    places = lax.axis_size("seq")
    segments = lax.axis_size("segment")
    rows = queries.shape[1]
    groups = group_count(queries.shape[2] // HD, places)
    inner = places // groups

    def swap(value, bits):
        return lax.ppermute(value, "seq", [(i, i ^ bits) for i in range(places)])

    def exchange(pieces):
        far = [swap(pieces[s], s * inner) for s in range(groups - 1, 0, -1)]
        return [pieces[0]] + far[::-1]

    def gather(parts):
        blocks, bits = list(parts), inner // 2
        while bits > 1:
            blocks = blocks + [swap(block, bits) for block in blocks]
            bits //= 2
        return blocks

    def with_other_core(blocks):
        return blocks + [swap(block, 1) for block in blocks] if inner > 1 else blocks

    width = queries.shape[2] // groups
    first, second = split_heads(queries, key_value, groups, inner)
    first, second = exchange(first), exchange(second)

    def near_and_far(pieces):
        halves = (pieces[: groups // 2], pieces[groups // 2 :])
        return [jnp.concatenate(some, axis=0) for some in halves if some]

    key_blocks = with_other_core(
        [jnp.concatenate(gather(near_and_far(first)), axis=0)]
    )
    parts = near_and_far([piece[:, :width] for piece in second])
    blocks = gather(parts)
    count = len(parts)
    value_blocks = with_other_core(
        [
            jnp.concatenate(blocks[i : i + count], axis=0)
            for i in range(0, len(blocks), count)
        ]
    )
    weights, sums = weigh(second, key_blocks, width)
    own = average(weights, sums, value_blocks, groups, 0, 1, [])
    near_by = average(weights, sums, value_blocks, groups, 1, groups // 2, own)
    rest = average(weights, sums, value_blocks, groups, groups // 2, groups, near_by)
    attended = own + near_by + rest

    def hand(value, step):
        pairs = [
            (
                segment * places + i,
                ((segment + 1) % segments) * places + (i ^ (step * inner)),
            )
            for segment in range(segments)
            for i in range(places)
        ]
        return lax.ppermute(value, ("segment", "seq"), pairs)

    handed = [hand(attended[s], s) for s in range(groups)]
    return join_heads(handed, inner)


def solution(mesh):
    return jax.shard_map(
        shards,
        mesh=mesh,
        in_specs=(P("segment", "seq", None), P(None, "segment", "seq", None)),
        out_specs=P("segment", "seq", None),
        check_vma=False,
    )
```
